32 devices in a mesh: sec: 4 (over y, x), dom: 8 (over z, core).
Axes of the slice: x: 2, y: 2, z: 4, core: 2. Of those that a mesh axis runs over, the one named last changes fastest.
Arguments:
- state_init: float32 [4, 8, 6, 1536], P('sec', 'dom'), may hold values from -6 to 6
- right_side: float32 [4, 8, 6, 1536], P('sec', 'dom'), may hold values from -6 to 6
- diag_inverse: float32 [4, 8, 6, 6, 1536], P('sec', 'dom'), may hold values from -1.2 to 2, as said below
- face_block: bfloat16 [4, 8, 6, 6, 9216], P('sec', 'dom'), may hold values from -0.47851562 to 0.47851562
- face_target: int32 [4, 8, 9216], P('sec', 'dom'), may hold values from 0 to 1535
- face_source: int32 [4, 8, 9216], P('sec', 'dom'), may hold values from 0 to 3071, as said below
- face_count: int32 [4, 8], P('sec', 'dom'), may hold values from 4608 to 9216, as said below
- send_list: int32 [4, 8, 1536], P('sec', 'dom'), may hold values from 0 to 1535
- surf_cell: int32 [4, 8, 128], P('sec', 'dom'), may hold values from 0 to 1535
- surf_count: int32 [4, 8, 8], P('sec', 'dom'), may hold values from 0 to 16, as said below
- surf_map: float32 [4, 8, 3, 6, 128], P('sec', 'dom'), may hold values from -3 to 3
- surf_node: int32 [3, 8, 128], P(None, 'dom'), may hold values from 0 to 1535
Outputs:
- state_final: float32 [4, 8, 6, 1536], P('sec', 'dom')
The draws below stay inside these ranges and needn't reach their ends.
Inputs may be any that keep to these rules, and one draw needn't show every extreme that they name: `face_source`: values below 1536 name the partition's own cells; a value 1536 + r * 192 + k names slot k of neighbour block r, which comes from partition d - offset r of the same section; only existing partitions are read, and each block is read in a leading run of its slots whose length differs from block to block; some block's run is 192 long. Only the first face_count entries of a partition's face lists are live; some partition lists 9216 live entries. Live slots of a flow partition towards structure partition o are its first surf_count slots of that block. Only some flow partitions (those at the wall, drawn from the seed) have live slots, each towards a few structure partitions of consecutive index (mod 8); some pair has 16 live slots. The structure section's row is zero and not read. `diag_inverse`: each block is a transposed block inverse; its diagonal entries are positive.
All inputs are finite; a program needn't handle non-finite values.
Results may differ from the reference program's by a relative error of at most 0.0003.
Values sent between devices are 32-bit elements; how exact they have to be, the bound alone decides.
A program may use at most 128 MiB of HBM per device.

```python
import jax
import jax.numpy as jnp
from jax import lax

NVAR = 6
NLOAD = 3
NBR = 8
CELLS = 1536
HCAP = 192
CAP = 16
ITERS = 2
FACES = 9216
GHOSTS = 1536
SLOTS = 128
N_SEC = 4
N_DOM = 8


neighbour_offsets = (1, -1, 2, -2, 3, -3, 4, -4)


def neighbour_counts(key):
    subkeys = jax.random.split(jax.random.fold_in(key, 20), 2)
    dims = (N_SEC, N_DOM, NBR)
    counts = jax.random.randint(subkeys[0], dims, 1, HCAP + 1)
    offsets = jnp.array(neighbour_offsets, dtype=jnp.int32)
    senders = jnp.arange(N_DOM, dtype=jnp.int32)[None, :, None] - offsets[None, None, :]
    exists = (senders >= 0) & (senders < N_DOM)
    fullest = jax.random.randint(subkeys[1], (), 1, N_DOM)
    forced = (jnp.arange(N_DOM, dtype=jnp.int32)[None, :, None] == fullest) & (jnp.arange(NBR, dtype=jnp.int32)[None, None, :] == 0)
    counts = jnp.where(forced, HCAP, counts)
    return jnp.where(exists, counts, 0).astype(jnp.int32)


def draw_face_source(key, part):
    counts = neighbour_counts(key)
    subkeys = jax.random.split(jax.random.fold_in(key, 11), 4)
    dims = (N_SEC, N_DOM, FACES)
    local_cells = jax.random.randint(subkeys[0], dims, 0, CELLS)
    block = jax.random.randint(subkeys[1], dims, 0, NBR)
    block_count = jnp.take_along_axis(counts, block, axis=2)
    slot = jax.random.randint(subkeys[2], dims, 0, 1048576) % jnp.maximum(block_count, 1)
    ghost_cells = CELLS + block * HCAP + slot
    chooser = jax.random.randint(subkeys[3], dims, 0, 6)
    return jnp.where((chooser == 0) & (block_count > 0), ghost_cells, local_cells).astype(jnp.int32)


def draw_face_count(key, part):
    subkeys = jax.random.split(jax.random.fold_in(key, 12), 2)
    initial = jax.random.randint(subkeys[0], (N_SEC, N_DOM), FACES // 2, FACES + 1)
    fullest = jax.random.randint(subkeys[1], (), 0, N_SEC * N_DOM)
    flat_index = jnp.arange(N_SEC * N_DOM, dtype=jnp.int32).reshape(N_SEC, N_DOM)
    return jnp.where(flat_index == fullest, FACES, initial).astype(jnp.int32)


def draw_surf_count(key, part):
    subkeys = jax.random.split(jax.random.fold_in(key, 13), 7)
    dims = (N_SEC, N_DOM, N_DOM)
    initial = jax.random.randint(subkeys[0], dims, 1, CAP + 1)
    at_wall = jax.random.randint(subkeys[1], (N_SEC, N_DOM), 0, 4) == 0
    first_owner = jax.random.randint(subkeys[2], (N_SEC, N_DOM), 0, N_DOM)
    reach = jax.random.randint(subkeys[3], (N_SEC, N_DOM), 2, 5)
    owners = jnp.arange(N_DOM, dtype=jnp.int32)[None, None, :]
    coupled = (owners - first_owner[:, :, None]) % N_DOM < reach[:, :, None]
    pick_sec = jax.random.randint(subkeys[4], (), 0, N_SEC - 1)
    pick_dom = jax.random.randint(subkeys[5], (), 0, N_DOM)
    sec_ids = jnp.arange(N_SEC, dtype=jnp.int32)[:, None]
    dom_ids = jnp.arange(N_DOM, dtype=jnp.int32)[None, :]
    chosen = (sec_ids == pick_sec) & (dom_ids == pick_dom)
    at_wall = at_wall | chosen
    forced = chosen[:, :, None] & (owners == first_owner[:, :, None])
    counts = jnp.where(forced, CAP, initial)
    flow_rows = (jnp.arange(N_SEC, dtype=jnp.int32) < N_SEC - 1)[:, None, None]
    live = at_wall[:, :, None] & coupled & flow_rows
    return jnp.where(live, counts, 0).astype(jnp.int32)


def draw_diag_inverse(key, part):
    subkeys = jax.random.split(jax.random.fold_in(key, 14), 2)
    scales = jnp.exp(jax.random.uniform(subkeys[0], (N_SEC, N_DOM, NVAR, CELLS), jnp.float32, jnp.log(0.2), jnp.log(2.0)))
    noise = jnp.clip(jax.random.normal(subkeys[1], (N_SEC, N_DOM, NVAR, NVAR, CELLS), jnp.float32), -3.0, 3.0)
    roots = jnp.sqrt(scales)
    outer = roots[:, :, :, None, :] * roots[:, :, None, :, :]
    identity = (jnp.arange(NVAR)[:, None] == jnp.arange(NVAR)[None, :]).astype(jnp.float32)[None, None, :, :, None]
    diagonal = scales[:, :, :, None, :] * identity
    return (diagonal + (1.0 - identity) * 0.2 * outer * noise).astype(jnp.float32)


def place_ends(values, stream_key, low, top_value):
    shape = values.shape
    index_at = [jax.random.randint(jax.random.fold_in(stream_key, axis), (), 0, shape[axis]) for axis in range(len(shape))]
    values = values.at[tuple(index_at)].set(low)
    longest = shape.index(max(shape))
    index_at[longest] = (index_at[longest] + 1) % shape[longest]
    return values.at[tuple(index_at)].set(top_value)


def level_of(rng, shape, cuts, low, high):
    factor_of = 1.0
    for axis_at, blocks in cuts:
        heights = jax.random.uniform(jax.random.fold_in(jax.random.fold_in(rng, 6), axis_at), (blocks,), jnp.float32, low / len(cuts), high / len(cuts))
        factor_of = factor_of * jnp.repeat(jnp.exp(heights), shape[axis_at] // blocks).reshape((-1,) + (1,) * (len(shape) - 1 - axis_at))
    return factor_of


def gaussian(own_key, shape, scale, limit, cuts=(), kind=jnp.bfloat16):
    result = jax.random.normal(own_key, shape, jnp.float32) * scale
    if len(cuts) > 0:
        result = level_of(own_key, shape, cuts, -0.22, 0.18) * result
    return jnp.clip(result, min=-limit, max=limit).astype(kind)


def setup_inputs(seed: int = 0) -> dict:
    streams_of = jax.random.split(jax.random.key(seed), 13)
    state_init = gaussian(streams_of[0], (N_SEC, N_DOM, NVAR, CELLS), 1.0, 6.0, ((0, 4), (1, 8)), jnp.float32)
    right_side = gaussian(streams_of[1], (N_SEC, N_DOM, NVAR, CELLS), 1.0, 6.0, ((0, 4), (1, 8)), jnp.float32)
    diag_inverse = draw_diag_inverse(jax.random.fold_in(streams_of[12], 71), 0)
    face_block = gaussian(streams_of[3], (N_SEC, N_DOM, NVAR, NVAR, FACES), 0.08, 0.47851562, ((0, 4), (1, 8)))
    face_target = place_ends(jax.random.randint(streams_of[4], (N_SEC, N_DOM, FACES), 0, CELLS), jax.random.fold_in(streams_of[4], 1), 0, CELLS - 1).astype(jnp.int32)
    face_source = draw_face_source(jax.random.fold_in(streams_of[12], 71), 0)
    face_count = draw_face_count(jax.random.fold_in(streams_of[12], 71), 0)
    send_list = place_ends(jax.random.randint(streams_of[7], (N_SEC, N_DOM, GHOSTS), 0, CELLS), jax.random.fold_in(streams_of[7], 1), 0, CELLS - 1).astype(jnp.int32)
    surf_cell = place_ends(jax.random.randint(streams_of[8], (N_SEC, N_DOM, SLOTS), 0, CELLS), jax.random.fold_in(streams_of[8], 1), 0, CELLS - 1).astype(jnp.int32)
    surf_count = draw_surf_count(jax.random.fold_in(streams_of[12], 71), 0)
    surf_map = gaussian(streams_of[10], (N_SEC, N_DOM, NLOAD, NVAR, SLOTS), 0.5, 3.0, ((0, 4), (1, 8)), jnp.float32)
    surf_node = place_ends(jax.random.randint(streams_of[11], (N_SEC - 1, N_DOM, SLOTS), 0, CELLS), jax.random.fold_in(streams_of[11], 1), 0, CELLS - 1).astype(jnp.int32)
    return dict(state_init=state_init, right_side=right_side, diag_inverse=diag_inverse, face_block=face_block, face_target=face_target, face_source=face_source, face_count=face_count, send_list=send_list, surf_cell=surf_cell, surf_count=surf_count, surf_map=surf_map, surf_node=surf_node)


neighbour_offsets = (1, -1, 2, -2, 3, -3, 4, -4)


def apply_blocks(blocks, vector):
    width = blocks.shape[-2]
    total = blocks[..., :, 0, :].astype(jnp.float32) * vector[..., 0:1, :]
    for column in range(1, width):
        total = total + blocks[..., :, column, :].astype(jnp.float32) * vector[..., column:column + 1, :]
    return total


def apply_transposed(blocks, vector):
    height = blocks.shape[-3]
    total = blocks[..., 0, :, :].astype(jnp.float32) * vector[..., 0:1, :]
    for row_index in range(1, height):
        total = total + blocks[..., row_index, :, :].astype(jnp.float32) * vector[..., row_index:row_index + 1, :]
    return total


def take_columns(matrix, indices):
    return matrix[:, indices]


select_nested = jax.vmap(jax.vmap(take_columns))


def scatter_columns(values, indices):
    return jnp.zeros((values.shape[0], CELLS), jnp.float32).at[:, indices].add(values)


scatter_nested = jax.vmap(jax.vmap(scatter_columns))


def face_sum(packed):
    extended, blocks, targets, sources, live_mask = packed
    gathered = extended[:, sources]
    contrib = apply_blocks(blocks, gathered) * live_mask[None, :]
    return jnp.zeros((NVAR, CELLS), jnp.float32).at[:, targets].add(contrib)


def load_into(node_ids, values):
    flat_ids = node_ids.reshape(-1)
    flat_values = jnp.transpose(values, (1, 0, 2)).reshape(NLOAD, -1)
    return jnp.zeros((NLOAD, CELLS), jnp.float32).at[:, flat_ids].add(flat_values)


def shift_partitions(piece, offset):
    blank = jnp.zeros((piece.shape[0], abs(offset)) + piece.shape[2:], jnp.float32)
    if offset > 0:
        return jnp.concatenate([blank, piece[:, :N_DOM - offset]], axis=1)
    return jnp.concatenate([piece[:, -offset:], blank], axis=1)


def reference(state_init, right_side, diag_inverse, face_block, face_target, face_source, face_count, send_list, surf_cell, surf_count, surf_map, surf_node):
    final_row = N_SEC - 1
    ghost_total = NBR * HCAP
    slot_total = N_DOM * CAP
    face_live = (jnp.arange(FACES, dtype=jnp.int32)[None, None, :] < face_count[:, :, None]).astype(jnp.float32)
    slot_live = (jnp.arange(CAP, dtype=jnp.int32)[None, None, None, :] < surf_count[:, :, :, None]).astype(jnp.float32)
    flow_flag = (jnp.arange(N_SEC, dtype=jnp.int32) < final_row).astype(jnp.float32)
    slot_live = slot_live.reshape(N_SEC, N_DOM, slot_total) * flow_flag[:, None, None]
    partitions = N_SEC * N_DOM
    state = state_init
    for sweep in range(ITERS):
        outgoing = select_nested(state, send_list).reshape(N_SEC, N_DOM, NVAR, NBR, HCAP)
        received = [shift_partitions(outgoing[:, :, :, index, :], neighbour_offsets[index]) for index in range(NBR)]
        ghosts = jnp.stack(received, axis=3).reshape(N_SEC, N_DOM, NVAR, ghost_total)
        extended = jnp.concatenate([state, ghosts], axis=3)
        face_terms = lax.map(face_sum, (
            extended.reshape(partitions, NVAR, CELLS + ghost_total),
            face_block.reshape(partitions, NVAR, NVAR, FACES),
            face_target.reshape(partitions, FACES),
            face_source.reshape(partitions, FACES),
            face_live.reshape(partitions, FACES))).reshape(N_SEC, N_DOM, NVAR, CELLS)
        loads = apply_blocks(surf_map, select_nested(state, surf_cell)) * slot_live[:, :, None, :]
        arrived = loads[:final_row].reshape(final_row, N_DOM, NLOAD, N_DOM, CAP)
        arrived = jnp.transpose(arrived, (0, 3, 2, 1, 4)).reshape(final_row, N_DOM, NLOAD, slot_total)
        load_total = jax.vmap(load_into, in_axes=(1, 1))(surf_node, arrived)
        struct_disp = state[final_row, :, :NLOAD, :]
        looked = jax.vmap(jax.vmap(take_columns, in_axes=(None, 0)), in_axes=(0, 1), out_axes=1)(struct_disp, surf_node)
        returned = looked.reshape(final_row, N_DOM, NLOAD, N_DOM, CAP)
        returned = jnp.transpose(returned, (0, 3, 2, 1, 4)).reshape(final_row, N_DOM, NLOAD, slot_total)
        returned = returned * slot_live[:final_row, :, None, :]
        pushed = apply_transposed(surf_map[:final_row], returned)
        flow_coupling = scatter_nested(pushed, surf_cell[:final_row])
        struct_coupling = jnp.concatenate([load_total, jnp.zeros((N_DOM, NVAR - NLOAD, CELLS), jnp.float32)], axis=1)
        coupling = jnp.concatenate([flow_coupling, struct_coupling[None]], axis=0)
        state = apply_blocks(diag_inverse, right_side - face_terms - coupling)
    return state
```

```python
import functools

import jax
import jax.numpy as jnp
from jax import lax
from jax.experimental import pallas as pl
from jax.experimental.pallas import tpu as pltpu
from jax.sharding import PartitionSpec as P

NVAR = 6
NLOAD = 3
NBR = 8
ITERS = 2
LANES = 128
ROWS = 8
LOW = 256
CHUNK = 512

neighbour_offsets = (1, -1, 2, -2, 3, -3, 4, -4)

F32 = jnp.float32
BF16 = jnp.bfloat16


def lane_gather(table, index):
    return jnp.take_along_axis(table, index, axis=1, mode="promise_in_bounds")


def spread(row):
    return jnp.broadcast_to(row, (ROWS, row.shape[-1]))


def gather_tiles(tiles, high, low):
    total = jnp.zeros((ROWS, LANES), F32)
    for at, tile in enumerate(tiles):
        total = jnp.where(high == at, lane_gather(tile, low), total)
    return total


def sum_rows(parts):
    width = parts[0].shape[1]
    row = lax.broadcasted_iota(jnp.int32, (ROWS, width), 0)
    parts = list(parts) + [None] * (ROWS - len(parts))
    step = ROWS // 2
    while step >= 1:
        upper = (row & step) == 0
        merged = []
        for at in range(step):
            a, b = parts[at], parts[at + step]
            if a is None and b is None:
                merged.append(None)
                continue
            if b is None:
                kept, moved = jnp.where(upper, a, 0.0), jnp.where(upper, 0.0, a)
            else:
                kept, moved = jnp.where(upper, a, b), jnp.where(upper, b, a)
            if step == ROWS // 2:
                moved = pltpu.roll(moved, step, 0)
            else:
                moved = jnp.where(upper, pltpu.roll(moved, ROWS - step, 0), pltpu.roll(moved, step, 0))
            merged.append(kept + moved)
        parts = merged
        step //= 2
    return parts[0]


def pad_rows(value):
    return jnp.concatenate([value, jnp.zeros((ROWS - value.shape[0], value.shape[1]), value.dtype)], axis=0)


def kernel(
    dims,
    state_init,
    right_side,
    inverse,
    face_block,
    face_target,
    face_source,
    face_count,
    send_list,
    surf_cell,
    surf_count,
    surf_map,
    surf_node,
    out_ref,
    state_buf,
    out_buf,
    halo_recv,
    ghost_buf,
    gath,
    onehot,
    load_send,
    load_recv,
    disp_send,
    disp_recv,
    halo_send_sem,
    halo_recv_sem,
    surf_send_sem,
    load_recv_sem,
    disp_recv_sem,
):
    n_sec, n_dom, cells, faces, slots, ghosts = dims
    flow = n_sec - 1
    tiles = cells // LANES
    ghost_tiles = ghosts // LANES
    block_slots = ghosts // NBR
    surf_tiles = slots // LANES
    cap = slots // n_dom
    per_tile = LANES // cap
    highs = cells // LOW
    sec = lax.axis_index("sec")
    dom = lax.axis_index("dom")
    is_structure = sec == flow
    lane = lax.broadcasted_iota(jnp.int32, (ROWS, LANES), 1)
    lane_block = lane // cap

    def present(offset):
        target = dom + offset
        return (target >= 0) & (target < n_dom)

    halo_recv[...] = jnp.zeros(halo_recv.shape, F32)
    load_recv[...] = jnp.zeros(load_recv.shape, F32)
    disp_recv[...] = jnp.zeros(disp_recv.shape, F32)

    barrier = pltpu.get_barrier_semaphore()
    for offset in neighbour_offsets:

        @pl.when(present(offset))
        def _():
            pl.semaphore_signal(barrier, inc=1, device_id={"dom": dom + offset})

    @pl.when(is_structure)
    def _():
        @pl.loop(0, flow * n_dom)
        def _(at):
            pl.semaphore_signal(barrier, inc=1, device_id={"sec": at // n_dom, "dom": at % n_dom})

    @pl.when(jnp.logical_not(is_structure))
    def _():
        @pl.loop(0, n_dom)
        def _(at):
            pl.semaphore_signal(barrier, inc=1, device_id={"sec": flow, "dom": at})

    expected = jnp.where(is_structure, flow * n_dom, n_dom)
    for offset in neighbour_offsets:
        expected = expected + present(offset).astype(jnp.int32)

    state_buf[...] = pad_rows(state_init[0, 0])
    live_faces = face_count[0, 0]

    def piece_tiles(index):
        start, end = index * block_slots, (index + 1) * block_slots
        return start, end, start // LANES, (end + LANES - 1) // LANES

    def halo_copy(sweep, index):
        _, _, first, last = piece_tiles(index)
        width = (last - first) * LANES
        return pltpu.make_async_remote_copy(
            src_ref=out_buf.at[sweep, :, pl.ds(first * LANES, width)],
            dst_ref=halo_recv.at[sweep, index, :, pl.ds(0, width)],
            send_sem=halo_send_sem.at[sweep, index],
            recv_sem=halo_recv_sem.at[sweep, index],
            device_id={"dom": dom + neighbour_offsets[index]},
        )

    def live_mask(tile):
        limit = jnp.zeros((ROWS, LANES), jnp.int32)
        for part in range(per_tile):
            limit = jnp.where(lane_block == part, surf_count[0, 0, tile * per_tile + part], limit)
        return (lane % cap) < limit

    def state_tiles():
        return [state_buf[:, at * LANES : (at + 1) * LANES] for at in range(tiles)]

    def prepare(sweep):
        own = state_tiles()
        for at in range(ghost_tiles):
            index = spread(send_list[0, :, at * LANES : (at + 1) * LANES])
            out_buf[sweep, :, at * LANES : (at + 1) * LANES] = gather_tiles(own, index // LANES, index % LANES)

    def prepare_surface(sweep):
        own = state_tiles()

        @pl.when(is_structure)
        def _():
            for section in range(flow):
                for tile in range(surf_tiles):
                    index = spread(surf_node[section, :, tile * LANES : (tile + 1) * LANES])
                    disp_send[sweep, section, tile] = gather_tiles(own, index // LANES, index % LANES)

        @pl.when(jnp.logical_not(is_structure))
        def _():
            for tile in range(surf_tiles):
                columns = slice(tile * LANES, (tile + 1) * LANES)
                index = spread(surf_cell[0, :, columns])
                values = gather_tiles(own, index // LANES, index % LANES)
                loads = sum_rows([pad_rows(surf_map[0, 0, row, :, columns] * values[:NVAR]) for row in range(NLOAD)])
                loads = jnp.where(live_mask(tile), loads, 0.0)
                mine = dom % per_tile
                for part in range(per_tile):
                    shift = lax.rem(mine - part + per_tile, per_tile) * cap
                    moved = pltpu.roll(loads, shift, 1)
                    load_send[sweep, tile * per_tile + part] = jnp.where(lane_block == mine, moved, 0.0)

    def send_halo(sweep):
        for index in range(NBR):

            @pl.when(present(neighbour_offsets[index]))
            def _():
                halo_copy(sweep, index).start()

    def send_surface(sweep):
        @pl.when(is_structure)
        def _():
            @pl.loop(0, flow * n_dom)
            def _(at):
                section, part = at // n_dom, at % n_dom
                pltpu.make_async_remote_copy(
                    src_ref=disp_send.at[sweep, section, part // per_tile],
                    dst_ref=disp_recv.at[sweep, dom],
                    send_sem=surf_send_sem.at[sweep],
                    recv_sem=disp_recv_sem.at[sweep],
                    device_id={"sec": section, "dom": part},
                ).start()

        @pl.when(jnp.logical_not(is_structure))
        def _():
            @pl.loop(0, n_dom)
            def _(at):
                pltpu.make_async_remote_copy(
                    src_ref=load_send.at[sweep, at],
                    dst_ref=load_recv.at[sweep, sec * n_dom + dom],
                    send_sem=surf_send_sem.at[sweep],
                    recv_sem=load_recv_sem.at[sweep],
                    device_id={"sec": flow, "dom": at},
                ).start()

    def build_onehot():
        step = CHUNK
        low_row = lax.broadcasted_iota(jnp.int32, (LOW, step), 0)

        @pl.loop(0, faces // step)
        def _(at):
            columns = pl.ds(pl.multiple_of(at * step, step), step)
            low = face_target[0, :, columns] % LOW
            onehot[:, columns] = jnp.where(low_row == low, 1.0, 0.0).astype(BF16)

    def local_gather():
        own = state_tiles()

        @pl.loop(0, faces // CHUNK)
        def _(at):
            for piece in range(CHUNK // LANES):
                columns = pl.ds(pl.multiple_of(at * CHUNK + piece * LANES, LANES), LANES)
                index = spread(face_source[0, :, columns])
                gath[:, columns] = gather_tiles(own, index // LANES, index % LANES)

    def receive_halo(sweep):
        for index in range(NBR):

            @pl.when(present(-neighbour_offsets[index]))
            def _():
                halo_copy(sweep, index).wait_recv()

        for at in range(ghost_tiles):
            total = jnp.zeros((ROWS, LANES), F32)
            for index in range(NBR):
                start, end, first, last = piece_tiles(index)
                if first <= at < last:
                    inside = (lane + at * LANES >= start) & (lane + at * LANES < end)
                    part = halo_recv[sweep, index, :, (at - first) * LANES : (at - first + 1) * LANES]
                    total = jnp.where(inside, part, total)
            ghost_buf[:, at * LANES : (at + 1) * LANES] = total

    def masked_dot(values, high, rhs):
        first = values.astype(BF16)
        second = (values - first.astype(F32)).astype(BF16)
        both = jnp.concatenate([first, second], axis=0)
        high = jnp.broadcast_to(high.astype(F32), both.shape).astype(BF16)
        lhs = jnp.concatenate(
            [jnp.where(high == at, both, jnp.zeros_like(both)) for at in range(highs)], axis=0
        )
        return lax.dot_general(lhs, rhs, (((1,), (1,)), ((), ())), preferred_element_type=F32)

    def face_pass():
        remote = [ghost_buf[:, at * LANES : (at + 1) * LANES] for at in range(ghost_tiles)]

        def step(at, total):
            base = at * CHUNK
            columns = pl.ds(pl.multiple_of(base, CHUNK), CHUNK)
            pieces = []
            for piece in range(CHUNK // LANES):
                part = pl.ds(pl.multiple_of(base + piece * LANES, LANES), LANES)
                index = spread(face_source[0, :, part])
                high, low = index // LANES, index % LANES
                value = gath[:, part]
                for tile in range(ghost_tiles):
                    value = jnp.where(high == tiles + tile, lane_gather(remote[tile], low), value)
                products = [
                    pad_rows(face_block[0, 0, row, :, part].astype(F32) * value[:NVAR]) for row in range(NVAR)
                ]
                pieces.append(sum_rows(products))
            contrib = jnp.concatenate(pieces, axis=1)
            entry = lax.broadcasted_iota(jnp.int32, (1, CHUNK), 1) + base
            high = jnp.where(entry < live_faces, face_target[0, :, columns] // LOW, highs)
            return total + masked_dot(contrib, high, onehot[:, columns])

        return lax.fori_loop(0, faces // CHUNK, step, jnp.zeros((2 * ROWS * highs, LOW), F32))

    def surface_pass(sweep):
        @pl.when(is_structure)
        def _():
            pltpu.make_async_copy(load_recv.at[sweep], load_recv.at[sweep], load_recv_sem.at[sweep]).wait()

        @pl.when(jnp.logical_not(is_structure))
        def _():
            pltpu.make_async_copy(disp_recv.at[sweep], disp_recv.at[sweep], disp_recv_sem.at[sweep]).wait()

        total = None
        low_row = lax.broadcasted_iota(jnp.int32, (LOW, LANES), 0)
        mine = dom % per_tile
        for section in range(flow):
            for tile in range(surf_tiles):
                columns = slice(tile * LANES, (tile + 1) * LANES)
                values = jnp.zeros((ROWS, LANES), F32)
                for part in range(per_tile):
                    values = values + load_recv[sweep, section * n_dom + tile * per_tile + part]
                cell = surf_node[section, :, columns]
                if section == 0:
                    back = jnp.zeros((ROWS, LANES), F32)
                    for part in range(per_tile):
                        shift = lax.rem(part - mine + per_tile, per_tile) * cap
                        moved = pltpu.roll(disp_recv[sweep, tile * per_tile + part], shift, 1)
                        back = jnp.where(lane_block == part, moved, back)
                    back = jnp.where(live_mask(tile), back, 0.0)
                    pushed = surf_map[0, 0, 0, :, columns] * back[0:1]
                    for row in range(1, NLOAD):
                        pushed = pushed + surf_map[0, 0, row, :, columns] * back[row : row + 1]
                    values = jnp.where(is_structure, values, pad_rows(pushed))
                    cell = jnp.where(is_structure, cell, surf_cell[0, :, columns])
                else:
                    values = jnp.where(is_structure, values, 0.0)
                rhs = jnp.where(low_row == cell % LOW, 1.0, 0.0).astype(BF16)
                term = masked_dot(values, cell // LOW, rhs)
                total = term if total is None else total + term
        return total

    prepare(0)
    prepare_surface(0)
    build_onehot()
    pl.semaphore_wait(barrier, expected)
    for sweep in range(ITERS):
        if sweep > 0:
            prepare(sweep)
            prepare_surface(sweep)
        send_halo(sweep)
        send_surface(sweep)
        local_gather()
        receive_halo(sweep)
        total = face_pass()
        total = total + surface_pass(sweep)
        for high in range(highs):
            base = 2 * ROWS * high
            columns = slice(high * LOW, (high + 1) * LOW)
            gone = total[base : base + ROWS] + total[base + ROWS : base + 2 * ROWS]
            rest = right_side[0, 0, :, columns] - gone[:NVAR]
            fresh = sum_rows([pad_rows(inverse[0, 0, row, :, columns] * rest) for row in range(NVAR)])
            if sweep == ITERS - 1:
                out_ref[0, 0, :, columns] = fresh[:NVAR]
            else:
                state_buf[:, columns] = fresh

    for sweep in range(ITERS):
        for index in range(NBR):

            @pl.when(present(neighbour_offsets[index]))
            def _():
                halo_copy(sweep, index).wait_send()

        @pl.when(is_structure)
        def _():
            pltpu.make_async_copy(load_recv.at[sweep], load_recv.at[sweep], surf_send_sem.at[sweep]).wait()

        @pl.when(jnp.logical_not(is_structure))
        def _():
            pltpu.make_async_copy(disp_recv.at[sweep], disp_recv.at[sweep], surf_send_sem.at[sweep]).wait()


def body(n_sec, n_dom, *args):
    cells = args[0].shape[-1]
    faces = args[4].shape[-1]
    ghosts = args[7].shape[-1]
    slots = args[8].shape[-1]
    flow = n_sec - 1
    piece = (2 * LANES - 1 + ghosts // NBR) // LANES * LANES
    vmem = pl.BlockSpec(memory_space=pltpu.VMEM)
    smem = pl.BlockSpec(memory_space=pltpu.SMEM)
    specs = [vmem] * 12
    specs[6] = smem
    specs[9] = smem
    return pl.pallas_call(
        functools.partial(kernel, (n_sec, n_dom, cells, faces, slots, ghosts)),
        out_shape=jax.ShapeDtypeStruct(args[0].shape, F32),
        in_specs=specs,
        out_specs=vmem,
        scratch_shapes=[
            pltpu.VMEM((ROWS, cells), F32),
            pltpu.VMEM((ITERS, ROWS, ghosts), F32),
            pltpu.VMEM((ITERS, NBR, ROWS, piece), F32),
            pltpu.VMEM((ROWS, ghosts), F32),
            pltpu.VMEM((ROWS, faces), F32),
            pltpu.VMEM((LOW, faces), BF16),
            pltpu.VMEM((ITERS, n_dom, ROWS, LANES), F32),
            pltpu.VMEM((ITERS, flow * n_dom, ROWS, LANES), F32),
            pltpu.VMEM((ITERS, flow, slots // LANES, ROWS, LANES), F32),
            pltpu.VMEM((ITERS, n_dom, ROWS, LANES), F32),
            pltpu.SemaphoreType.DMA((ITERS, NBR)),
            pltpu.SemaphoreType.DMA((ITERS, NBR)),
            pltpu.SemaphoreType.DMA((ITERS,)),
            pltpu.SemaphoreType.DMA((ITERS,)),
            pltpu.SemaphoreType.DMA((ITERS,)),
        ],
        compiler_params=pltpu.CompilerParams(
            collective_id=0, has_side_effects=True, vmem_limit_bytes=48 * 1024 * 1024
        ),
    )(*args)


def solution(mesh):
    in_specs = (
        P("sec", "dom", None, None),
        P("sec", "dom", None, None),
        P("sec", "dom", None, None, None),
        P("sec", "dom", None, None, None),
        P("sec", "dom", None),
        P("sec", "dom", None),
        P("sec", "dom"),
        P("sec", "dom", None),
        P("sec", "dom", None),
        P("sec", "dom", None),
        P("sec", "dom", None, None, None),
        P(None, "dom", None),
    )
    out_specs = P("sec", "dom", None, None)
    run = functools.partial(body, mesh.shape["sec"], mesh.shape["dom"])
    return jax.shard_map(run, mesh=mesh, in_specs=in_specs, out_specs=out_specs, check_vma=False)
```

```python
import functools

import jax
import jax.numpy as jnp
from jax import lax
from jax.experimental import pallas as pl
from jax.experimental.pallas import tpu as pltpu
from jax.sharding import PartitionSpec as P

NVAR = 6
NLOAD = 3
NBR = 8
ITERS = 2
LANES = 128
ROWS = 8
LOW = 256
WIDE = 256
CHUNK = 3072

neighbour_offsets = (1, -1, 2, -2, 3, -3, 4, -4)

F32 = jnp.float32
BF16 = jnp.bfloat16


def lane_gather(table, index):
    return jnp.take_along_axis(table, index, axis=1, mode="promise_in_bounds")


def spread(row):
    return jnp.broadcast_to(row, (ROWS, row.shape[-1]))


def gather_tiles(tiles, high, low):
    total = jnp.zeros((ROWS, LANES), F32)
    for at, tile in enumerate(tiles):
        total = jnp.where(high == at, lane_gather(tile, low), total)
    return total


def sum_rows(parts):
    width = parts[0].shape[1]
    row = lax.broadcasted_iota(jnp.int32, (ROWS, width), 0)
    parts = list(parts) + [None] * (ROWS - len(parts))
    step = ROWS // 2
    while step >= 1:
        upper = (row & step) == 0
        merged = []
        for at in range(step):
            a, b = parts[at], parts[at + step]
            if a is None and b is None:
                merged.append(None)
                continue
            if b is None:
                kept, moved = jnp.where(upper, a, 0.0), jnp.where(upper, 0.0, a)
            else:
                kept, moved = jnp.where(upper, a, b), jnp.where(upper, b, a)
            if step == ROWS // 2:
                moved = pltpu.roll(moved, step, 0)
            else:
                moved = jnp.where(upper, pltpu.roll(moved, ROWS - step, 0), pltpu.roll(moved, step, 0))
            merged.append(kept + moved)
        parts = merged
        step //= 2
    return parts[0]


def pad_rows(value):
    return jnp.concatenate([value, jnp.zeros((ROWS - value.shape[0], value.shape[1]), value.dtype)], axis=0)


def kernel(
    dims,
    state_init,
    right_side,
    inverse,
    face_block,
    face_target,
    face_source,
    face_count,
    send_list,
    surf_cell,
    surf_count,
    surf_map,
    surf_node,
    out_ref,
    init_v,
    right_v,
    inverse_v,
    block_v,
    target_v,
    source_v,
    list_v,
    cell_v,
    map_v,
    node_v,
    state_buf,
    state_lhs,
    ghost_lhs,
    out_hot,
    source_hot,
    out_buf,
    halo_recv,
    ghost_buf,
    gath,
    onehot,
    load_send,
    load_recv,
    disp_send,
    disp_recv,
    halo_send_sem,
    halo_recv_sem,
    surf_send_sem,
    load_recv_sem,
    disp_recv_sem,
    fetch_sem,
    ready_sem,
):
    n_sec, n_dom, cells, faces, slots, ghosts = dims
    flow = n_sec - 1
    tiles = cells // LANES
    ghost_tiles = ghosts // LANES
    block_slots = ghosts // NBR
    surf_tiles = slots // LANES
    cap = slots // n_dom
    per_tile = LANES // cap
    highs = cells // LOW
    sec = lax.axis_index("sec")
    dom = lax.axis_index("dom")
    is_structure = sec == flow
    lane = lax.broadcasted_iota(jnp.int32, (ROWS, LANES), 1)
    lane_block = lane // cap

    def present(offset):
        target = dom + offset
        return (target >= 0) & (target < n_dom)

    order = (
        (state_init, init_v),
        (send_list, list_v),
        (surf_node, node_v),
        (surf_cell, cell_v),
        (surf_map, map_v),
        (face_source, source_v),
        (face_target, target_v),
        (face_block, block_v),
        (right_side, right_v),
        (inverse, inverse_v),
    )
    fetches = [pltpu.make_async_copy(src, dst, fetch_sem.at[at]) for at, (src, dst) in enumerate(order)]
    for fetch in fetches:
        fetch.start()

    halo_recv[...] = jnp.zeros(halo_recv.shape, F32)
    load_recv[...] = jnp.zeros(load_recv.shape, F32)
    disp_recv[...] = jnp.zeros(disp_recv.shape, F32)

    barrier = pltpu.get_barrier_semaphore()

    @pl.loop(0, n_dom)
    def _(at):
        @pl.when(at != dom)
        def _():
            pl.semaphore_signal(barrier, inc=1, device_id={"dom": at})

    def greet(sem):
        @pl.when(is_structure)
        def _():
            for section in range(flow):
                pl.semaphore_signal(sem, inc=1, device_id={"sec": section})

        @pl.when(jnp.logical_not(is_structure))
        def _():
            pl.semaphore_signal(sem, inc=1, device_id={"sec": flow})

    greet(barrier)
    partners = jnp.where(is_structure, flow, 1)

    live_faces = face_count[0, 0]

    def piece_tiles(index):
        start, end = index * block_slots, (index + 1) * block_slots
        return start, end, start // LANES, (end + LANES - 1) // LANES

    def halo_copy(sweep, index):
        _, _, first, last = piece_tiles(index)
        width = (last - first) * LANES
        return pltpu.make_async_remote_copy(
            src_ref=out_buf.at[sweep, :, pl.ds(first * LANES, width)],
            dst_ref=halo_recv.at[sweep, index, :, pl.ds(0, width)],
            send_sem=halo_send_sem.at[sweep, index],
            recv_sem=halo_recv_sem.at[sweep, index],
            device_id={"dom": dom + neighbour_offsets[index]},
        )

    sub = lax.broadcasted_iota(jnp.int32, (ROWS, LANES), 0)
    block_lane = sub * cap + lane % cap

    def pack(values):
        packed = jnp.zeros((ROWS, LANES), F32)
        for row in range(NLOAD):
            packed = jnp.where(lane_block == row, lane_gather(spread(values[row : row + 1]), block_lane), packed)
        return packed

    def unpack(rows):
        values = jnp.zeros((ROWS, LANES), F32)
        for part, row in enumerate(rows):
            values = jnp.where(lane_block == part, lane_gather(spread(row), block_lane), values)
        return values

    def two_terms(values):
        first = values.astype(BF16)
        second = (values - first.astype(F32)).astype(BF16)
        return jnp.concatenate([first, second], axis=0)

    def picked(lhs, hot, high, first_high, value):
        found = lax.dot_general(lhs, hot, (((1,), (0,)), ((), ())), preferred_element_type=F32)
        for at in range(lhs.shape[0] // (2 * ROWS)):
            base = 2 * ROWS * at
            part = found[base : base + ROWS] + found[base + ROWS : base + 2 * ROWS]
            value = jnp.where(high == first_high + at, part, value)
        return value

    def set_state_lhs():
        for at in range(cells // WIDE):
            state_lhs[2 * ROWS * at : 2 * ROWS * (at + 1)] = two_terms(state_buf[:, at * WIDE : (at + 1) * WIDE])

    def live_mask(tile):
        limit = jnp.zeros((ROWS, LANES), jnp.int32)
        for part in range(per_tile):
            limit = jnp.where(lane_block == part, surf_count[0, 0, tile * per_tile + part], limit)
        return (lane % cap) < limit

    def state_tiles():
        return [state_buf[:, at * LANES : (at + 1) * LANES] for at in range(tiles)]

    def prepare(sweep):
        for at in range(ghosts // WIDE):
            columns = slice(at * WIDE, (at + 1) * WIDE)
            high = spread(list_v[0, :, columns]) // WIDE
            start = jnp.zeros((ROWS, WIDE), F32)
            out_buf[sweep, :, columns] = picked(state_lhs[...], out_hot[:, columns], high, 0, start)

    def map_rows(row, tile):
        if surf_tiles == 1:
            return map_v[row * NVAR : (row + 1) * NVAR, :]
        return map_v[pl.ds(row * NVAR * surf_tiles + tile, NVAR, stride=surf_tiles), :]

    def prepare_surface(sweep):
        own = state_tiles()

        @pl.when(is_structure)
        def _():
            for section in range(flow):
                for tile in range(surf_tiles):
                    index = spread(node_v[section, :, tile * LANES : (tile + 1) * LANES])
                    packed = pack(gather_tiles(own, index // LANES, index % LANES))
                    for part in range(per_tile):
                        disp_send[sweep, section * n_dom + tile * per_tile + part] = packed[part : part + 1]

        @pl.when(jnp.logical_not(is_structure))
        def _():
            for tile in range(surf_tiles):
                columns = slice(tile * LANES, (tile + 1) * LANES)
                index = spread(cell_v[0, :, columns])
                values = gather_tiles(own, index // LANES, index % LANES)
                loads = sum_rows([pad_rows(map_rows(row, tile) * values[:NVAR]) for row in range(NLOAD)])
                packed = pack(jnp.where(live_mask(tile), loads, 0.0))
                for part in range(per_tile):
                    load_send[sweep, tile * per_tile + part] = packed[part : part + 1]

    def send_halo(sweep):
        for index in range(NBR):

            @pl.when(present(neighbour_offsets[index]))
            def _():
                halo_copy(sweep, index).start()

    def send_surface(sweep):
        @pl.when(is_structure)
        def _():
            @pl.loop(0, flow * n_dom)
            def _(at):
                section, part = at // n_dom, at % n_dom
                pltpu.make_async_remote_copy(
                    src_ref=disp_send.at[sweep, at],
                    dst_ref=disp_recv.at[sweep, dom],
                    send_sem=surf_send_sem.at[sweep],
                    recv_sem=disp_recv_sem.at[sweep],
                    device_id={"sec": section, "dom": part},
                ).start()

        @pl.when(jnp.logical_not(is_structure))
        def _():
            @pl.loop(0, n_dom)
            def _(at):
                pltpu.make_async_remote_copy(
                    src_ref=load_send.at[sweep, at],
                    dst_ref=load_recv.at[sweep, sec * n_dom + dom],
                    send_sem=surf_send_sem.at[sweep],
                    recv_sem=load_recv_sem.at[sweep],
                    device_id={"sec": flow, "dom": at},
                ).start()

    def one_hot(low, rows):
        row = lax.broadcasted_iota(jnp.int32, (rows, low.shape[1]), 0)
        return jnp.where(row == low, 1.0, 0.0).astype(BF16)

    def build_list_hot():
        for at in range(ghosts // WIDE):
            columns = slice(at * WIDE, (at + 1) * WIDE)
            out_hot[:, columns] = one_hot(list_v[0, :, columns] % WIDE, WIDE)

    def build_source_hot():
        @pl.loop(0, faces // CHUNK)
        def _(at):
            columns = pl.ds(pl.multiple_of(at * CHUNK, CHUNK), CHUNK)
            source_hot[:, columns] = one_hot(source_v[0, :, columns] % WIDE, WIDE)

    def build_target_hot():
        @pl.loop(0, faces // CHUNK)
        def _(at):
            columns = pl.ds(pl.multiple_of(at * CHUNK, CHUNK), CHUNK)
            onehot[:, columns] = one_hot(target_v[0, :, columns] % LOW, LOW)

    def local_gather():
        @pl.loop(0, faces // CHUNK)
        def _(at):
            columns = pl.ds(pl.multiple_of(at * CHUNK, CHUNK), CHUNK)
            high = spread(source_v[0, :, columns]) // WIDE
            start = jnp.zeros((ROWS, CHUNK), F32)
            gath[:, columns] = picked(state_lhs[...], source_hot[:, columns], high, 0, start)

    def receive_halo(sweep):
        for index in range(NBR):

            @pl.when(present(-neighbour_offsets[index]))
            def _():
                halo_copy(sweep, index).wait_recv()

        for at in range(ghost_tiles):
            total = jnp.zeros((ROWS, LANES), F32)
            for index in range(NBR):
                start, end, first, last = piece_tiles(index)
                if first <= at < last:
                    inside = (lane + at * LANES >= start) & (lane + at * LANES < end)
                    part = halo_recv[sweep, index, :, (at - first) * LANES : (at - first + 1) * LANES]
                    total = jnp.where(inside, part, total)
            ghost_buf[:, at * LANES : (at + 1) * LANES] = total
        for at in range(ghosts // WIDE):
            ghost_lhs[2 * ROWS * at : 2 * ROWS * (at + 1)] = two_terms(ghost_buf[:, at * WIDE : (at + 1) * WIDE])

    def masked_dot(values, high, rhs):
        both = two_terms(values)
        high = jnp.broadcast_to(high.astype(F32), both.shape).astype(BF16)
        lhs = jnp.concatenate(
            [jnp.where(high == at, both, jnp.zeros_like(both)) for at in range(highs)], axis=0
        )
        return lax.dot_general(lhs, rhs, (((1,), (1,)), ((), ())), preferred_element_type=F32)

    def face_pass():
        def step(at, total):
            base = at * CHUNK
            columns = pl.ds(pl.multiple_of(base, CHUNK), CHUNK)
            high = spread(source_v[0, :, columns]) // WIDE
            value = picked(ghost_lhs[...], source_hot[:, columns], high, cells // WIDE, gath[:, columns])
            pieces = []
            for piece in range(CHUNK // LANES):
                part = pl.ds(pl.multiple_of(base + piece * LANES, LANES), LANES)
                here = value[:NVAR, piece * LANES : (piece + 1) * LANES]
                pieces.append(
                    sum_rows([pad_rows(block_v[0, 0, row, :, part].astype(F32) * here) for row in range(NVAR)])
                )
            contrib = jnp.concatenate(pieces, axis=1)
            entry = lax.broadcasted_iota(jnp.int32, (1, CHUNK), 1) + base
            high = jnp.where(entry < live_faces, target_v[0, :, columns] // LOW, highs)
            return total + masked_dot(contrib, high, onehot[:, columns])

        return lax.fori_loop(0, faces // CHUNK, step, jnp.zeros((2 * ROWS * highs, LOW), F32))

    def surface_pass(sweep):
        @pl.when(is_structure)
        def _():
            pltpu.make_async_copy(load_recv.at[sweep], load_recv.at[sweep], load_recv_sem.at[sweep]).wait()

        @pl.when(jnp.logical_not(is_structure))
        def _():
            pltpu.make_async_copy(disp_recv.at[sweep], disp_recv.at[sweep], disp_recv_sem.at[sweep]).wait()

        total = None
        for section in range(flow):
            for tile in range(surf_tiles):
                columns = slice(tile * LANES, (tile + 1) * LANES)
                first = section * n_dom + tile * per_tile
                values = unpack([load_recv[sweep, first + part] for part in range(per_tile)])
                cell = node_v[section, :, columns]
                if section == 0:
                    back = unpack([disp_recv[sweep, tile * per_tile + part] for part in range(per_tile)])
                    back = jnp.where(live_mask(tile), back, 0.0)
                    pushed = map_rows(0, tile) * back[0:1]
                    for row in range(1, NLOAD):
                        pushed = pushed + map_rows(row, tile) * back[row : row + 1]
                    values = jnp.where(is_structure, values, pad_rows(pushed))
                    cell = jnp.where(is_structure, cell, cell_v[0, :, columns])
                else:
                    values = jnp.where(is_structure, values, 0.0)
                term = masked_dot(values, cell // LOW, one_hot(cell % LOW, LOW))
                total = term if total is None else total + term
        return total

    fetches[0].wait()
    for at in range(tiles):
        state_buf[:, at * LANES : (at + 1) * LANES] = pad_rows(init_v[pl.ds(at, NVAR, stride=tiles), :])
    set_state_lhs()
    fetches[1].wait()
    build_list_hot()
    prepare(0)
    pl.semaphore_wait(barrier, n_dom - 1 + partners)
    greet(ready_sem)
    send_halo(0)
    for fetch in fetches[2:6]:
        fetch.wait()
    prepare_surface(0)
    build_source_hot()
    pl.semaphore_wait(ready_sem, partners)
    send_surface(0)
    fetches[6].wait()
    build_target_hot()
    for fetch in fetches[7:]:
        fetch.wait()
    for sweep in range(ITERS):
        if sweep > 0:
            prepare(sweep)
            send_halo(sweep)
            prepare_surface(sweep)
            send_surface(sweep)
        local_gather()
        receive_halo(sweep)
        total = face_pass()
        total = total + surface_pass(sweep)
        for at in range(tiles):
            base = 2 * ROWS * (at * LANES // LOW)
            columns = slice(at * LANES % LOW, at * LANES % LOW + LANES)
            gone = total[base : base + ROWS, columns] + total[base + ROWS : base + 2 * ROWS, columns]
            rest = right_v[pl.ds(at, NVAR, stride=tiles), :] - gone[:NVAR]
            fresh = sum_rows(
                [
                    pad_rows(inverse_v[pl.ds(row * NVAR * tiles + at, NVAR, stride=tiles), :] * rest)
                    for row in range(NVAR)
                ]
            )
            if sweep == ITERS - 1:
                out_ref[pl.ds(at, NVAR, stride=tiles), :] = fresh[:NVAR]
            else:
                state_buf[:, at * LANES : (at + 1) * LANES] = fresh
        if sweep < ITERS - 1:
            set_state_lhs()

    for sweep in range(ITERS):
        for index in range(NBR):

            @pl.when(present(neighbour_offsets[index]))
            def _():
                halo_copy(sweep, index).wait_send()

        @pl.when(is_structure)
        def _():
            pltpu.make_async_copy(load_recv.at[sweep], load_recv.at[sweep], surf_send_sem.at[sweep]).wait()

        @pl.when(jnp.logical_not(is_structure))
        def _():
            pltpu.make_async_copy(disp_recv.at[sweep], disp_recv.at[sweep], surf_send_sem.at[sweep]).wait()


def body(n_sec, n_dom, *args):
    cells = args[0].shape[-1]
    faces = args[4].shape[-1]
    ghosts = args[7].shape[-1]
    slots = args[8].shape[-1]
    flow = n_sec - 1
    piece = (2 * LANES - 1 + ghosts // NBR) // LANES * LANES
    vmem = pl.BlockSpec(memory_space=pltpu.VMEM)
    smem = pl.BlockSpec(memory_space=pltpu.SMEM)
    specs = [pl.BlockSpec(memory_space=pltpu.HBM)] * 12
    specs[6] = smem
    specs[9] = smem
    args = list(args)
    for at in (0, 1, 2, 10):
        args[at] = args[at].reshape(-1, LANES)
    fetched = [args[at] for at in (0, 1, 2, 3, 4, 5, 7, 8, 10, 11)]
    wide_rows = 2 * ROWS * (cells // WIDE)
    ghost_rows = 2 * ROWS * (ghosts // WIDE)
    out = pl.pallas_call(
        functools.partial(kernel, (n_sec, n_dom, cells, faces, slots, ghosts)),
        out_shape=jax.ShapeDtypeStruct(args[0].shape, F32),
        in_specs=specs,
        out_specs=vmem,
        scratch_shapes=[
            *[pltpu.VMEM(value.shape, value.dtype) for value in fetched],
            pltpu.VMEM((ROWS, cells), F32),
            pltpu.VMEM((wide_rows, WIDE), BF16),
            pltpu.VMEM((ghost_rows, WIDE), BF16),
            pltpu.VMEM((WIDE, ghosts), BF16),
            pltpu.VMEM((WIDE, faces), BF16),
            pltpu.VMEM((ITERS, ROWS, ghosts), F32),
            pltpu.VMEM((ITERS, NBR, ROWS, piece), F32),
            pltpu.VMEM((ROWS, ghosts), F32),
            pltpu.VMEM((ROWS, faces), F32),
            pltpu.VMEM((LOW, faces), BF16),
            pltpu.VMEM((ITERS, n_dom, 1, LANES), F32),
            pltpu.VMEM((ITERS, flow * n_dom, 1, LANES), F32),
            pltpu.VMEM((ITERS, flow * n_dom, 1, LANES), F32),
            pltpu.VMEM((ITERS, n_dom, 1, LANES), F32),
            pltpu.SemaphoreType.DMA((ITERS, NBR)),
            pltpu.SemaphoreType.DMA((ITERS, NBR)),
            pltpu.SemaphoreType.DMA((ITERS,)),
            pltpu.SemaphoreType.DMA((ITERS,)),
            pltpu.SemaphoreType.DMA((ITERS,)),
            pltpu.SemaphoreType.DMA((len(fetched),)),
            pltpu.SemaphoreType.REGULAR,
        ],
        compiler_params=pltpu.CompilerParams(
            collective_id=0, has_side_effects=True, vmem_limit_bytes=63 * 1024 * 1024 + 768 * 1024
        ),
    )(*args)
    return out.reshape(1, 1, NVAR, cells)


def solution(mesh):
    in_specs = (
        P("sec", "dom", None, None),
        P("sec", "dom", None, None),
        P("sec", "dom", None, None, None),
        P("sec", "dom", None, None, None),
        P("sec", "dom", None),
        P("sec", "dom", None),
        P("sec", "dom"),
        P("sec", "dom", None),
        P("sec", "dom", None),
        P("sec", "dom", None),
        P("sec", "dom", None, None, None),
        P(None, "dom", None),
    )
    out_specs = P("sec", "dom", None, None)
    run = functools.partial(body, mesh.shape["sec"], mesh.shape["dom"])
    return jax.shard_map(run, mesh=mesh, in_specs=in_specs, out_specs=out_specs, check_vma=False)
```
